32 devices in a mesh: sta: 4 (over y, x), evt: 8 (over z, core).
Axes of the slice: x: 2, y: 2, z: 4, core: 2. Of those that a mesh axis runs over, the one named last changes fastest.
Arguments:
- traces: bfloat16 [3, 32, 512, 2048], P(None, 'sta', 'evt'), may hold values from -96 to 96
- baz_bin: int32 [32, 512], P('sta', 'evt'), may hold values from 0 to 35
- inc_bin: int32 [32, 512], P('sta', 'evt'), may hold values from 0 to 7
- counts: int32 [32], P('sta'), may hold values from 64 to 512
- depth_index: int32 [32, 512], P('sta'), may hold values from 0 to 2046
- tile_of: int32 [32], replicated, may hold values from 0 to 15
Outputs:
- stack: float32 [16, 5, 2, 512], P('sta', None, None, 'evt')
The draws below stay inside these ranges and needn't reach their ends.
All inputs are finite; a program needn't handle non-finite values.
Results may differ from the reference program's by a relative error of at most 0.0003.
Values sent between devices are 32-bit elements; how exact they have to be, the bound alone decides.
A program may use at most 64 MiB of HBM per device.

```python
import jax
import jax.numpy as jnp
from jax import lax

NS = 2048
DEPTHS = 512
BAZ_BINS = 36
INC_BINS = 8
STATIONS = 32
EVENTS = 512
TILES = 16


def set_ends(result, own_key, low, top_value):
    longest = result.shape.index(max(result.shape))
    spots = []
    for shift in (0, 1):
        where = [jax.random.randint(jax.random.fold_in(own_key, axis), (), 0, length) for axis, length in enumerate(result.shape)]
        where[longest] = (where[longest] + shift) % result.shape[longest]
        spots.append(tuple(where))
    return result.at[spots[0]].set(low).at[spots[1]].set(top_value)


def block_scale(stream_key, dims, shards, low, high):
    factor_of = 1.0
    for dim, parts in shards:
        steps = jax.random.uniform(jax.random.fold_in(jax.random.fold_in(stream_key, 6), dim), (parts,), jnp.float32, low / len(shards), high / len(shards))
        factor_of = factor_of * jnp.repeat(jnp.exp(steps), dims[dim] // parts).reshape((-1,) + (1,) * (len(dims) - 1 - dim))
    return factor_of


def centred(own_key, shape, deviation, bound, shards=(), kind=jnp.bfloat16):
    result = deviation * jax.random.normal(own_key, shape, jnp.float32)
    if shards:
        result = result * block_scale(own_key, shape, shards, -0.22, 0.18)
    return jnp.clip(result, -bound, bound).astype(kind)


def setup_inputs(seed: int = 0) -> dict:
    key_of = jax.random.split(jax.random.key(seed), 7)
    return {
        "traces": centred(key_of[0], (3, STATIONS, EVENTS, NS), 16.0, 96.0, ((1, 4), (2, 8))),
        "baz_bin": set_ends(jax.random.randint(key_of[1], (STATIONS, EVENTS), 0, BAZ_BINS), jax.random.fold_in(key_of[1], 1), 0, BAZ_BINS - 1).astype(jnp.int32),
        "inc_bin": set_ends(jax.random.randint(key_of[2], (STATIONS, EVENTS), 0, INC_BINS), jax.random.fold_in(key_of[2], 1), 0, INC_BINS - 1).astype(jnp.int32),
        "counts": set_ends(jax.random.randint(key_of[3], (STATIONS,), EVENTS // 8, EVENTS + 1), jax.random.fold_in(key_of[3], 1), EVENTS // 8, EVENTS).astype(jnp.int32),
        "depth_index": set_ends(jax.random.randint(key_of[4], (STATIONS, DEPTHS), 0, NS - 1), jax.random.fold_in(key_of[4], 1), 0, (NS - 1) - 1).astype(jnp.int32),
        "tile_of": set_ends(jax.random.randint(key_of[5], (STATIONS,), 0, TILES), jax.random.fold_in(key_of[5], 1), 0, TILES - 1).astype(jnp.int32),
    }


def reference(traces, baz_bin, inc_bin, counts, depth_index, tile_of):
    highest = lax.Precision.HIGHEST

    def one_station(station):
        block = lax.dynamic_index_in_dim(traces, station, 1, keepdims=False).astype(jnp.float32)
        bins = lax.dynamic_index_in_dim(baz_bin, station, 0, keepdims=False)
        tilts = lax.dynamic_index_in_dim(inc_bin, station, 0, keepdims=False)
        total = lax.dynamic_index_in_dim(counts, station, 0, keepdims=False)
        indices = lax.dynamic_index_in_dim(depth_index, station, 0, keepdims=False).astype(jnp.int32)
        phi = (bins.astype(jnp.float32) + 0.5) * (2.0 * jnp.pi / BAZ_BINS)
        incidence = (12.0 + 2.5 * (tilts.astype(jnp.float32) + 0.5)) * (jnp.pi / 180.0)
        cosine = jnp.cos(phi)[:, None]
        sine = jnp.sin(phi)[:, None]
        radial = -(cosine * block[1] + sine * block[2])
        quality = jnp.cos(incidence)[:, None] * radial + jnp.sin(incidence)[:, None] * block[0]
        transverse = sine * block[1] - cosine * block[2]
        data = jnp.concatenate([quality, transverse], axis=1)
        live = (jnp.arange(EVENTS) < total).astype(jnp.float32)
        harm = jnp.stack([jnp.ones_like(phi), jnp.cos(phi), jnp.sin(phi), jnp.cos(2.0 * phi), jnp.sin(2.0 * phi)], axis=1)
        weighted = harm * live[:, None]
        normal = jnp.dot(weighted.T, harm, precision=highest) + jnp.eye(5, dtype=jnp.float32)
        rhs = jnp.dot(weighted.T, data, precision=highest)
        coeff = jnp.linalg.solve(normal, rhs).reshape(5, 2, NS)
        return 0.5 * (coeff[:, :, indices] + coeff[:, :, indices + 1])
    profiles = lax.map(one_station, jnp.arange(STATIONS))
    onehot = (tile_of[None, :] == jnp.arange(TILES)[:, None]).astype(jnp.float32)
    sums = jnp.einsum('ts,skcz->tkcz', onehot, profiles, precision=highest)
    members = jnp.sum(onehot, axis=1)
    return sums / jnp.maximum(members, 1.0)[:, None, None, None]
```

```python
import functools

import jax
import jax.numpy as jnp
from jax import lax
from jax.experimental import pallas as pl
from jax.experimental.pallas import tpu as pltpu
from jax.sharding import PartitionSpec as P

BAZ_BINS = 36
HARMS = 5
LANES = 128
ROWS = 8
USED = 6
HALF = LANES // 2


def pick_lanes(values, lanes):
    return jnp.take_along_axis(values, lanes, axis=1, mode="promise_in_bounds")


def kernel(
    evt_count,
    sta_count,
    tiles,
    traces_ref,
    baz_ref,
    inc_ref,
    counts_ref,
    depth_ref,
    tile_ref,
    out_ref,
    trace_buf,
    weight_buf,
    normal_buf,
    send_buf,
    recv_buf,
    sum_buf,
    fit_buf,
    fit_recv,
    load_sem,
    send_sem,
    recv_sem,
    fit_send_sem,
    fit_recv_sem,
):
    stations, slots = baz_ref.shape
    samples = traces_ref.shape[3]
    depths = depth_ref.shape[1]
    share = depths // evt_count
    evt = lax.axis_index("evt")
    sta = lax.axis_index("sta")
    f32 = jnp.float32

    def load(s):
        return pltpu.make_async_copy(traces_ref.at[:, s], trace_buf.at[s], load_sem.at[s])

    for s in range(stations):
        load(s).start()
    barrier = pltpu.get_barrier_semaphore()
    for j in range(1, evt_count):
        pl.semaphore_signal(
            barrier, inc=1, device_id={"evt": lax.rem(evt + j, evt_count)},
            device_id_type=pl.DeviceIdType.MESH,
        )
    for j in range(1, sta_count):
        pl.semaphore_signal(
            barrier, inc=1, device_id={"sta": lax.rem(sta + j, sta_count)},
            device_id_type=pl.DeviceIdType.MESH,
        )

    phi = (baz_ref[...].astype(f32) + 0.5) * (2.0 * jnp.pi / BAZ_BINS)
    tilt = (12.0 + 2.5 * (inc_ref[...].astype(f32) + 0.5)) * (jnp.pi / 180.0)
    cosine, sine = jnp.cos(phi), jnp.sin(phi)
    cos_tilt, sin_tilt = jnp.cos(tilt), jnp.sin(tilt)
    row_ids = lax.broadcasted_iota(jnp.int32, (stations, slots), 0)
    total = jnp.zeros((stations, slots), jnp.int32)
    for s in range(stations):
        total = jnp.where(row_ids == s, counts_ref[s], total)
    slot_ids = evt * slots + lax.broadcasted_iota(jnp.int32, (stations, slots), 1)
    live = jnp.where(slot_ids < total, 1.0, 0.0).astype(f32)
    harm = [
        jnp.ones_like(phi),
        cosine,
        sine,
        2.0 * cosine * cosine - 1.0,
        2.0 * sine * cosine,
    ]
    weighted = [h * live for h in harm]
    parts = [
        [sin_tilt, -cos_tilt * cosine, -cos_tilt * sine],
        [jnp.zeros_like(phi), sine, -cosine],
    ]
    weight_buf[...] = jnp.zeros_like(weight_buf)
    for c in range(2):
        for k in range(HARMS):
            for m in range(3):
                weight_buf[c * ROWS + k, :, m * slots:(m + 1) * slots] = weighted[k] * parts[c][m]
    lane_ids = lax.broadcasted_iota(jnp.int32, (stations, LANES), 1)
    packed = jnp.zeros((stations, LANES), f32)
    place = 0
    for k in range(HARMS):
        for l in range(k + 1):
            column = jnp.sum(weighted[k] * harm[l], axis=1, keepdims=True)
            packed = jnp.where(lane_ids == place, column, packed)
            place += 1
    normal_buf[...] = packed

    pl.semaphore_wait(barrier, evt_count - 1 + sta_count - 1)

    def remote(j, s):
        target = lax.rem(evt + j, evt_count)
        return pltpu.make_async_remote_copy(
            src_ref=send_buf.at[target, s, 0:USED],
            dst_ref=recv_buf.at[j - 1, s, 0:USED],
            send_sem=send_sem.at[j - 1],
            recv_sem=recv_sem.at[j - 1],
            device_id={"evt": target},
            device_id_type=pl.DeviceIdType.MESH,
        )

    lane8 = lax.broadcasted_iota(jnp.int32, (ROWS, LANES), 1)
    row8 = lax.broadcasted_iota(jnp.int32, (ROWS, LANES), 0)

    def station(s, carry):
        load(s).wait()
        weights = weight_buf[:, s, :]
        high = weights.astype(jnp.bfloat16)
        low = (weights - high.astype(f32)).astype(jnp.bfloat16)
        block = trace_buf[s].reshape(3 * slots, samples)
        right = jnp.dot(
            jnp.concatenate([high, low], axis=0), block, preferred_element_type=f32
        )
        pair = right[0:2 * ROWS] + right[2 * ROWS:4 * ROWS]
        pair = 0.5 * (pair + pltpu.roll(pair, samples - 1, 1))
        first, second = pair[0:ROWS], pair[ROWS:2 * ROWS]
        normal_row = jnp.broadcast_to(normal_buf[pl.ds(s, 1), :], (ROWS, LANES))
        picks = depth_ref[pl.ds(s, 1), :]
        for z in range(depths // LANES):
            index = jnp.broadcast_to(picks[:, z * LANES:(z + 1) * LANES], (ROWS, LANES))
            chunk = lax.shift_right_logical(index, 7)
            lane = lax.bitwise_and(index, LANES - 1)
            got = [jnp.zeros((ROWS, LANES), f32)] * 2
            for n in range(samples // LANES):
                here = chunk == n
                for c, values in enumerate((first, second)):
                    taken = pick_lanes(values[:, n * LANES:(n + 1) * LANES], lane)
                    got[c] = jnp.where(here, taken, got[c])
            for d in range(LANES // share):
                left = got[0] if d == 0 else pltpu.roll(got[0], LANES - d * share, 1)
                move = (HALF - d * share) % LANES
                rest = got[1] if move == 0 else pltpu.roll(got[1], move, 1)
                both = jnp.where(lane8 < HALF, left, rest)
                send_buf[z * (LANES // share) + d, s] = jnp.where(row8 == HARMS, normal_row, both)
        for j in range(1, evt_count):
            remote(j, s).start()
        return carry

    lax.fori_loop(0, stations, station, 0)

    def whole(j):
        return pltpu.make_async_remote_copy(
            src_ref=send_buf.at[lax.rem(evt + j, evt_count), :, 0:USED],
            dst_ref=recv_buf.at[j - 1, :, 0:USED],
            send_sem=send_sem.at[j - 1],
            recv_sem=recv_sem.at[j - 1],
            device_id={"evt": lax.rem(evt + j, evt_count)},
            device_id_type=pl.DeviceIdType.MESH,
        )

    sums = send_buf[evt, :, 0:USED]
    for j in range(1, evt_count):
        whole(j).wait_recv()
        sums = sums + recv_buf[j - 1, :, 0:USED]
    sum_buf[:, 0:USED] = sums

    right = [sum_buf[:, k, :] for k in range(HARMS)]
    entries = sum_buf[:, HARMS, :]
    matrix = {}
    place = 0
    for k in range(HARMS):
        for l in range(k + 1):
            value = jnp.broadcast_to(entries[:, place:place + 1], (stations, LANES))
            matrix[k, l] = value + 1.0 if k == l else value
            place += 1
    inverse = []
    for p in range(HARMS):
        inverse.append(1.0 / matrix[p, p])
        for k in range(p + 1, HARMS):
            ratio = matrix[k, p] * inverse[p]
            for l in range(p + 1, k + 1):
                matrix[k, l] = matrix[k, l] - ratio * matrix[l, p]
            right[k] = right[k] - ratio * right[p]
    solved = [None] * HARMS
    for k in reversed(range(HARMS)):
        value = right[k]
        for l in range(k + 1, HARMS):
            value = value - matrix[l, k] * solved[l]
        solved[k] = value * inverse[k]
        fit_buf[k] = solved[k]

    def fits(j):
        return pltpu.make_async_remote_copy(
            src_ref=fit_buf,
            dst_ref=fit_recv.at[j - 1],
            send_sem=fit_send_sem.at[j - 1],
            recv_sem=fit_recv_sem.at[j - 1],
            device_id={"sta": lax.rem(sta + j, sta_count)},
            device_id_type=pl.DeviceIdType.MESH,
        )

    for j in range(1, sta_count):
        fits(j).start()

    ids = lax.broadcasted_iota(jnp.int32, (stations, LANES), 0)
    masks = []
    for j in range(sta_count):
        base = lax.rem(sta + sta_count - j, sta_count) * stations
        of = jnp.zeros((stations, LANES), jnp.int32)
        for s in range(stations):
            of = jnp.where(ids == s, tile_ref[base + s], of)
        masks.append(
            [jnp.where(of == sta * tiles + t, 1.0, 0.0).astype(f32) for t in range(tiles)]
        )
    scale = []
    for t in range(tiles):
        members = functools.reduce(jnp.add, [m[t] for m in masks])
        scale.append(jnp.maximum(jnp.sum(members, axis=0, keepdims=True), 1.0))
    stack = [[masks[0][t] * solved[k] for k in range(HARMS)] for t in range(tiles)]
    for j in range(1, sta_count):
        fits(j).wait_recv()
        for k in range(HARMS):
            value = fit_recv[j - 1, k]
            for t in range(tiles):
                stack[t][k] = stack[t][k] + masks[j][t] * value
    for t in range(tiles):
        for k in range(HARMS):
            row = jnp.sum(stack[t][k], axis=0, keepdims=True) / scale[t]
            out_ref[t, k, 0:1, :] = row[:, 0:share]
            out_ref[t, k, 1:2, :] = row[:, HALF:HALF + share]
    for j in range(1, evt_count):
        whole(j).wait_send()
    for j in range(1, sta_count):
        fits(j).wait_send()


def body(evt_count, sta_count, traces, baz_bin, inc_bin, counts, depth_index, tile_of):
    _, stations, slots, samples = traces.shape
    depths = depth_index.shape[1]
    share = depths // evt_count
    tiles = tile_count(tile_of.shape[0]) // sta_count
    vmem = pl.BlockSpec(memory_space=pltpu.VMEM)
    smem = pl.BlockSpec(memory_space=pltpu.SMEM)
    f32 = jnp.float32
    return pl.pallas_call(
        functools.partial(kernel, evt_count, sta_count, tiles),
        out_shape=jax.ShapeDtypeStruct((tiles, HARMS, 2, share), f32),
        in_specs=[pl.BlockSpec(memory_space=pl.ANY), vmem, vmem, smem, vmem, smem],
        out_specs=vmem,
        scratch_shapes=[
            pltpu.VMEM((stations, 3, slots, samples), traces.dtype),
            pltpu.VMEM((2 * ROWS, stations, 3 * slots), f32),
            pltpu.VMEM((stations, LANES), f32),
            pltpu.VMEM((evt_count, stations, ROWS, LANES), f32),
            pltpu.VMEM((evt_count - 1, stations, ROWS, LANES), f32),
            pltpu.VMEM((stations, ROWS, LANES), f32),
            pltpu.VMEM((HARMS, stations, LANES), f32),
            pltpu.VMEM((sta_count - 1, HARMS, stations, LANES), f32),
            pltpu.SemaphoreType.DMA((stations,)),
            pltpu.SemaphoreType.DMA((evt_count - 1,)),
            pltpu.SemaphoreType.DMA((evt_count - 1,)),
            pltpu.SemaphoreType.DMA((sta_count - 1,)),
            pltpu.SemaphoreType.DMA((sta_count - 1,)),
        ],
        compiler_params=pltpu.CompilerParams(collective_id=0, has_side_effects=True),
    )(traces, baz_bin, inc_bin, counts, depth_index, tile_of)


def tile_count(stations):
    return stations // 2


def solution(mesh):
    return jax.shard_map(
        functools.partial(body, mesh.shape["evt"], mesh.shape["sta"]),
        mesh=mesh,
        in_specs=(
            P(None, "sta", "evt", None),
            P("sta", "evt"),
            P("sta", "evt"),
            P("sta"),
            P("sta", None),
            P(),
        ),
        out_specs=P("sta", None, None, "evt"),
        check_vma=False,
    )
```

```python
import functools

import jax
import jax.numpy as jnp
from jax import lax
from jax.experimental import pallas as pl
from jax.experimental.pallas import tpu as pltpu
from jax.sharding import PartitionSpec as P

BAZ_BINS = 36
HARMS = 5
LANES = 128
ROWS = 8
USED = 6
HALF = LANES // 2
GROUP = 2


def pick_lanes(values, lanes):
    return jnp.take_along_axis(values, lanes, axis=1, mode="promise_in_bounds")


def kernel(
    evt_count,
    sta_count,
    tiles,
    traces_ref,
    baz_hbm,
    inc_hbm,
    counts_hbm,
    depth_hbm,
    tile_hbm,
    out_ref,
    trace_buf,
    baz_ref,
    inc_ref,
    counts_ref,
    depth_ref,
    tile_ref,
    weight_buf,
    normal_buf,
    send_buf,
    recv_buf,
    sum_buf,
    fit_buf,
    fit_recv,
    load_sem,
    small_sem,
    send_sem,
    recv_sem,
    fit_send_sem,
    fit_recv_sem,
):
    stations, slots = baz_ref.shape
    samples = traces_ref.shape[3]
    depths = depth_ref.shape[1]
    share = depths // evt_count
    evt = lax.axis_index("evt")
    sta = lax.axis_index("sta")
    f32 = jnp.float32

    def load(s):
        return pltpu.make_async_copy(traces_ref.at[:, s], trace_buf.at[s], load_sem.at[s])

    small = [
        pltpu.make_async_copy(src, dst, small_sem.at[n])
        for n, (src, dst) in enumerate(
            [
                (baz_hbm, baz_ref),
                (inc_hbm, inc_ref),
                (counts_hbm, counts_ref),
                (depth_hbm, depth_ref),
                (tile_hbm, tile_ref),
            ]
        )
    ]
    for copy in small:
        copy.start()
    for s in range(stations):
        load(s).start()
    barrier = pltpu.get_barrier_semaphore()
    for j in range(1, evt_count):
        pl.semaphore_signal(
            barrier, inc=1, device_id={"evt": lax.rem(evt + j, evt_count)},
            device_id_type=pl.DeviceIdType.MESH,
        )
    for j in range(1, sta_count):
        pl.semaphore_signal(
            barrier, inc=1, device_id={"sta": lax.rem(sta + j, sta_count)},
            device_id_type=pl.DeviceIdType.MESH,
        )

    for copy in small:
        copy.wait()

    phi = (baz_ref[...].astype(f32) + 0.5) * (2.0 * jnp.pi / BAZ_BINS)
    tilt = (12.0 + 2.5 * (inc_ref[...].astype(f32) + 0.5)) * (jnp.pi / 180.0)
    cosine, sine = jnp.cos(phi), jnp.sin(phi)
    cos_tilt, sin_tilt = jnp.cos(tilt), jnp.sin(tilt)
    row_ids = lax.broadcasted_iota(jnp.int32, (stations, slots), 0)
    total = jnp.zeros((stations, slots), jnp.int32)
    for s in range(stations):
        total = jnp.where(row_ids == s, counts_ref[s], total)
    slot_ids = evt * slots + lax.broadcasted_iota(jnp.int32, (stations, slots), 1)
    live = jnp.where(slot_ids < total, 1.0, 0.0).astype(f32)
    harm = [
        jnp.ones_like(phi),
        cosine,
        sine,
        2.0 * cosine * cosine - 1.0,
        2.0 * sine * cosine,
    ]
    weighted = [h * live for h in harm]
    parts = [
        [sin_tilt, -cos_tilt * cosine, -cos_tilt * sine],
        [jnp.zeros_like(phi), sine, -cosine],
    ]
    weight_buf[...] = jnp.zeros_like(weight_buf)
    for c in range(2):
        for k in range(HARMS):
            for m in range(3):
                weight_buf[c * ROWS + k, :, m * slots:(m + 1) * slots] = weighted[k] * parts[c][m]
    lane_ids = lax.broadcasted_iota(jnp.int32, (stations, LANES), 1)
    packed = jnp.zeros((stations, LANES), f32)
    place = 0
    for k in range(HARMS):
        for l in range(k + 1):
            column = jnp.sum(weighted[k] * harm[l], axis=1, keepdims=True)
            packed = jnp.where(lane_ids == place, column, packed)
            place += 1
    normal_buf[...] = packed

    def remote(j, s):
        target = lax.rem(evt + j, evt_count)
        return pltpu.make_async_remote_copy(
            src_ref=send_buf.at[target, pl.ds(s, GROUP), 0:USED],
            dst_ref=recv_buf.at[j - 1, pl.ds(s, GROUP), 0:USED],
            send_sem=send_sem.at[j - 1],
            recv_sem=recv_sem.at[j - 1],
            device_id={"evt": target},
            device_id_type=pl.DeviceIdType.MESH,
        )

    lane8 = lax.broadcasted_iota(jnp.int32, (ROWS, LANES), 1)
    row8 = lax.broadcasted_iota(jnp.int32, (ROWS, LANES), 0)

    def right_sides(s):
        weights = weight_buf[:, s, :]
        high = weights.astype(jnp.bfloat16)
        low = (weights - high.astype(f32)).astype(jnp.bfloat16)
        block = trace_buf[s].reshape(3 * slots, samples)
        right = jnp.dot(
            jnp.concatenate([high, low], axis=0), block, preferred_element_type=f32
        )
        pair = right[0:2 * ROWS] + right[2 * ROWS:4 * ROWS]
        return 0.5 * (pair + pltpu.roll(pair, samples - 1, 1))

    def pick(s, pair):
        first, second = pair[0:ROWS], pair[ROWS:2 * ROWS]
        normal_row = jnp.broadcast_to(normal_buf[pl.ds(s, 1), :], (ROWS, LANES))
        picks = depth_ref[pl.ds(s, 1), :]
        for z in range(depths // LANES):
            index = jnp.broadcast_to(picks[:, z * LANES:(z + 1) * LANES], (ROWS, LANES))
            chunk = lax.shift_right_logical(index, 7)
            lane = lax.bitwise_and(index, LANES - 1)
            got = [jnp.zeros((ROWS, LANES), f32)] * 2
            for n in range(samples // LANES):
                here = chunk == n
                for c, values in enumerate((first, second)):
                    taken = pick_lanes(values[:, n * LANES:(n + 1) * LANES], lane)
                    got[c] = jnp.where(here, taken, got[c])
            for d in range(LANES // share):
                left = got[0] if d == 0 else pltpu.roll(got[0], LANES - d * share, 1)
                move = (HALF - d * share) % LANES
                rest = got[1] if move == 0 else pltpu.roll(got[1], move, 1)
                both = jnp.where(lane8 < HALF, left, rest)
                send_buf[z * (LANES // share) + d, s] = jnp.where(row8 == HARMS, normal_row, both)

    def step(i, carry):
        at = i * GROUP
        for g in range(GROUP):
            load(at + g).wait()
        pairs = [right_sides(at + g) for g in range(GROUP)]
        for g in range(GROUP):
            pick(at + g, pairs[g])

        @pl.when(i == 0)
        def _():
            pl.semaphore_wait(barrier, evt_count - 1 + sta_count - 1)

        for j in range(1, evt_count):
            remote(j, at).start()
        return carry

    lax.fori_loop(0, stations // GROUP, step, 0)

    def whole(j):
        return pltpu.make_async_remote_copy(
            src_ref=send_buf.at[lax.rem(evt + j, evt_count), :, 0:USED],
            dst_ref=recv_buf.at[j - 1, :, 0:USED],
            send_sem=send_sem.at[j - 1],
            recv_sem=recv_sem.at[j - 1],
            device_id={"evt": lax.rem(evt + j, evt_count)},
            device_id_type=pl.DeviceIdType.MESH,
        )

    sums = send_buf[evt, :, 0:USED]
    for j in range(1, evt_count):
        whole(j).wait_recv()
        sums = sums + recv_buf[j - 1, :, 0:USED]
    sum_buf[:, 0:USED] = sums

    right = [sum_buf[:, k, :] for k in range(HARMS)]
    entries = sum_buf[:, HARMS, :]
    matrix = {}
    place = 0
    for k in range(HARMS):
        for l in range(k + 1):
            value = jnp.broadcast_to(entries[:, place:place + 1], (stations, LANES))
            matrix[k, l] = value + 1.0 if k == l else value
            place += 1
    inverse = []
    for p in range(HARMS):
        inverse.append(1.0 / matrix[p, p])
        for k in range(p + 1, HARMS):
            ratio = matrix[k, p] * inverse[p]
            for l in range(p + 1, k + 1):
                matrix[k, l] = matrix[k, l] - ratio * matrix[l, p]
            right[k] = right[k] - ratio * right[p]
    solved = [None] * HARMS
    for k in reversed(range(HARMS)):
        value = right[k]
        for l in range(k + 1, HARMS):
            value = value - matrix[l, k] * solved[l]
        solved[k] = value * inverse[k]
        fit_buf[k] = solved[k]

    def fits(j):
        return pltpu.make_async_remote_copy(
            src_ref=fit_buf,
            dst_ref=fit_recv.at[j - 1],
            send_sem=fit_send_sem.at[j - 1],
            recv_sem=fit_recv_sem.at[j - 1],
            device_id={"sta": lax.rem(sta + j, sta_count)},
            device_id_type=pl.DeviceIdType.MESH,
        )

    for j in range(1, sta_count):
        fits(j).start()

    ids = lax.broadcasted_iota(jnp.int32, (stations, LANES), 0)
    masks = []
    for j in range(sta_count):
        base = lax.rem(sta + sta_count - j, sta_count) * stations
        of = jnp.zeros((stations, LANES), jnp.int32)
        for s in range(stations):
            of = jnp.where(ids == s, tile_ref[base + s], of)
        masks.append(
            [jnp.where(of == sta * tiles + t, 1.0, 0.0).astype(f32) for t in range(tiles)]
        )
    scale = []
    for t in range(tiles):
        members = functools.reduce(jnp.add, [m[t] for m in masks])
        scale.append(jnp.maximum(jnp.sum(members, axis=0, keepdims=True), 1.0))
    stack = [[masks[0][t] * solved[k] for k in range(HARMS)] for t in range(tiles)]
    for j in range(1, sta_count):
        fits(j).wait_recv()
        for k in range(HARMS):
            value = fit_recv[j - 1, k]
            for t in range(tiles):
                stack[t][k] = stack[t][k] + masks[j][t] * value
    for t in range(tiles):
        for k in range(HARMS):
            row = jnp.sum(stack[t][k], axis=0, keepdims=True) / scale[t]
            out_ref[t, k, 0:1, :] = row[:, 0:share]
            out_ref[t, k, 1:2, :] = row[:, HALF:HALF + share]
    for j in range(1, evt_count):
        whole(j).wait_send()
    for j in range(1, sta_count):
        fits(j).wait_send()


def body(evt_count, sta_count, traces, baz_bin, inc_bin, counts, depth_index, tile_of):
    _, stations, slots, samples = traces.shape
    depths = depth_index.shape[1]
    share = depths // evt_count
    tiles = tile_count(tile_of.shape[0]) // sta_count
    vmem = pl.BlockSpec(memory_space=pltpu.VMEM)
    anywhere = pl.BlockSpec(memory_space=pl.ANY)
    f32 = jnp.float32
    return pl.pallas_call(
        functools.partial(kernel, evt_count, sta_count, tiles),
        out_shape=pltpu.VMEM((tiles, HARMS, 2, share), f32),
        in_specs=[anywhere] * 6,
        out_specs=vmem,
        scratch_shapes=[
            pltpu.VMEM((stations, 3, slots, samples), traces.dtype),
            pltpu.VMEM(baz_bin.shape, jnp.int32),
            pltpu.VMEM(inc_bin.shape, jnp.int32),
            pltpu.SMEM(counts.shape, jnp.int32),
            pltpu.VMEM(depth_index.shape, jnp.int32),
            pltpu.SMEM(tile_of.shape, jnp.int32),
            pltpu.VMEM((2 * ROWS, stations, 3 * slots), f32),
            pltpu.VMEM((stations, LANES), f32),
            pltpu.VMEM((evt_count, stations, ROWS, LANES), f32),
            pltpu.VMEM((evt_count - 1, stations, ROWS, LANES), f32),
            pltpu.VMEM((stations, ROWS, LANES), f32),
            pltpu.VMEM((HARMS, stations, LANES), f32),
            pltpu.VMEM((sta_count - 1, HARMS, stations, LANES), f32),
            pltpu.SemaphoreType.DMA((stations,)),
            pltpu.SemaphoreType.DMA((5,)),
            pltpu.SemaphoreType.DMA((evt_count - 1,)),
            pltpu.SemaphoreType.DMA((evt_count - 1,)),
            pltpu.SemaphoreType.DMA((sta_count - 1,)),
            pltpu.SemaphoreType.DMA((sta_count - 1,)),
        ],
        compiler_params=pltpu.CompilerParams(collective_id=0, has_side_effects=True),
    )(traces, baz_bin, inc_bin, counts, depth_index, tile_of)


def tile_count(stations):
    return stations // 2


def solution(mesh):
    return jax.shard_map(
        functools.partial(body, mesh.shape["evt"], mesh.shape["sta"]),
        mesh=mesh,
        in_specs=(
            P(None, "sta", "evt", None),
            P("sta", "evt"),
            P("sta", "evt"),
            P("sta"),
            P("sta", None),
            P(),
        ),
        out_specs=P("sta", None, None, "evt"),
        check_vma=False,
    )
```

```python
import functools

import jax
import jax.numpy as jnp
from jax import lax
from jax.experimental import pallas as pl
from jax.experimental.pallas import tpu as pltpu
from jax.sharding import PartitionSpec as P

BAZ_BINS = 36
HARMS = 5
LANES = 128
ROWS = 8
USED = HARMS
TERMS = 16
HALF = LANES // 2
GROUP = 2


def pick_lanes(values, lanes):
    return jnp.take_along_axis(values, lanes, axis=1, mode="promise_in_bounds")


def kernel(
    evt_count,
    sta_count,
    tiles,
    traces_ref,
    baz_hbm,
    inc_hbm,
    counts_hbm,
    depth_hbm,
    tile_hbm,
    out_ref,
    trace_buf,
    baz_ref,
    inc_ref,
    counts_ref,
    depth_ref,
    tile_ref,
    weight_buf,
    left_buf,
    normal_buf,
    normal_recv,
    send_buf,
    recv_buf,
    sum_buf,
    fit_buf,
    fit_recv,
    load_sem,
    small_sem,
    send_sem,
    recv_sem,
    normal_send_sem,
    normal_recv_sem,
    fit_send_sem,
    fit_recv_sem,
):
    stations, slots = baz_ref.shape
    samples = traces_ref.shape[3]
    depths = depth_ref.shape[1]
    share = depths // evt_count
    evt = lax.axis_index("evt")
    sta = lax.axis_index("sta")
    f32 = jnp.float32

    def load(s):
        return pltpu.make_async_copy(traces_ref.at[:, s], trace_buf.at[s], load_sem.at[s])

    small = [
        pltpu.make_async_copy(src, dst, small_sem.at[n])
        for n, (src, dst) in enumerate(
            [
                (baz_hbm, baz_ref),
                (inc_hbm, inc_ref),
                (counts_hbm, counts_ref),
                (depth_hbm, depth_ref),
                (tile_hbm, tile_ref),
            ]
        )
    ]
    for copy in small:
        copy.start()
    for s in range(stations):
        load(s).start()
    barrier = pltpu.get_barrier_semaphore()
    for j in range(1, evt_count):
        pl.semaphore_signal(
            barrier, inc=1, device_id={"evt": lax.rem(evt + j, evt_count)},
            device_id_type=pl.DeviceIdType.MESH,
        )
    for j in range(1, sta_count):
        pl.semaphore_signal(
            barrier, inc=1, device_id={"sta": lax.rem(sta + j, sta_count)},
            device_id_type=pl.DeviceIdType.MESH,
        )

    for copy in small:
        copy.wait()

    phi = (baz_ref[...].astype(f32) + 0.5) * (2.0 * jnp.pi / BAZ_BINS)
    tilt = (12.0 + 2.5 * (inc_ref[...].astype(f32) + 0.5)) * (jnp.pi / 180.0)
    cosine, sine = jnp.cos(phi), jnp.sin(phi)
    cos_tilt, sin_tilt = jnp.cos(tilt), jnp.sin(tilt)
    row_ids = lax.broadcasted_iota(jnp.int32, (stations, slots), 0)
    total = jnp.zeros((stations, slots), jnp.int32)
    for s in range(stations):
        total = jnp.where(row_ids == s, counts_ref[s], total)
    slot_ids = evt * slots + lax.broadcasted_iota(jnp.int32, (stations, slots), 1)
    live = jnp.where(slot_ids < total, 1.0, 0.0).astype(f32)
    harm = [
        jnp.ones_like(phi),
        cosine,
        sine,
        2.0 * cosine * cosine - 1.0,
        2.0 * sine * cosine,
    ]
    weighted = [h * live for h in harm]
    parts = [
        [sin_tilt, -cos_tilt * cosine, -cos_tilt * sine],
        [jnp.zeros_like(phi), sine, -cosine],
    ]
    weight_buf[...] = jnp.zeros_like(weight_buf)
    for c in range(2):
        for k in range(HARMS):
            at = (c * ROWS + k) * stations
            for m in range(3):
                lane = m * slots
                weight_buf[
                    lane // LANES, at:at + stations, lane % LANES:lane % LANES + slots
                ] = weighted[k] * parts[c][m]
    for s in range(stations):
        for n in range(weight_buf.shape[0]):
            weights = weight_buf[n, pl.ds(s, 2 * ROWS, stride=stations), :]
            high = weights.astype(jnp.bfloat16)
            low = (weights - high.astype(f32)).astype(jnp.bfloat16)
            left_buf[s, 0:2 * ROWS, n * LANES:(n + 1) * LANES] = high
            left_buf[s, 2 * ROWS:4 * ROWS, n * LANES:(n + 1) * LANES] = low
    lane_ids = lax.broadcasted_iota(jnp.int32, (stations, LANES), 1)
    station_ids = lax.broadcasted_iota(jnp.int32, (stations, LANES), 0)
    packed = jnp.zeros((stations, LANES), f32)
    place = 0
    for k in range(HARMS):
        for l in range(k + 1):
            column = jnp.sum(weighted[k] * harm[l], axis=1, keepdims=True)
            packed = jnp.where(lane_ids % TERMS == place, column, packed)
            place += 1
    packed = jnp.where(lane_ids // TERMS == station_ids, packed, 0.0)
    normal_buf[0:1] = jnp.sum(packed, axis=0, keepdims=True)

    def normals(j):
        return pltpu.make_async_remote_copy(
            src_ref=normal_buf.at[0:1],
            dst_ref=normal_recv.at[j - 1, 0:1],
            send_sem=normal_send_sem.at[j - 1],
            recv_sem=normal_recv_sem.at[j - 1],
            device_id={"evt": lax.rem(evt + j, evt_count)},
            device_id_type=pl.DeviceIdType.MESH,
        )

    def remote(j, s):
        target = lax.rem(evt + j, evt_count)
        return pltpu.make_async_remote_copy(
            src_ref=send_buf.at[target, pl.ds(s, GROUP), 0:USED],
            dst_ref=recv_buf.at[j - 1, pl.ds(s, GROUP), 0:USED],
            send_sem=send_sem.at[j - 1],
            recv_sem=recv_sem.at[j - 1],
            device_id={"evt": target},
            device_id_type=pl.DeviceIdType.MESH,
        )

    lane8 = lax.broadcasted_iota(jnp.int32, (ROWS, LANES), 1)

    def right_sides(s):
        block = trace_buf[s].reshape(3 * slots, samples)
        right = jnp.dot(left_buf[s, :, 0:3 * slots], block, preferred_element_type=f32)
        pair = right[0:2 * ROWS] + right[2 * ROWS:4 * ROWS]
        return 0.5 * (pair + pltpu.roll(pair, samples - 1, 1))

    def pick(s, pair):
        first, second = pair[0:ROWS], pair[ROWS:2 * ROWS]
        picks = depth_ref[pl.ds(s, 1), :]
        for z in range(depths // LANES):
            index = jnp.broadcast_to(picks[:, z * LANES:(z + 1) * LANES], (ROWS, LANES))
            chunk = lax.shift_right_logical(index, 7)
            lane = lax.bitwise_and(index, LANES - 1)
            got = [jnp.zeros((ROWS, LANES), f32)] * 2
            for n in range(samples // LANES):
                here = chunk == n
                for c, values in enumerate((first, second)):
                    taken = pick_lanes(values[:, n * LANES:(n + 1) * LANES], lane)
                    got[c] = jnp.where(here, taken, got[c])
            for d in range(LANES // share):
                left = got[0] if d == 0 else pltpu.roll(got[0], LANES - d * share, 1)
                move = (HALF - d * share) % LANES
                rest = got[1] if move == 0 else pltpu.roll(got[1], move, 1)
                send_buf[z * (LANES // share) + d, s] = jnp.where(lane8 < HALF, left, rest)

    def step(i, carry):
        at = i * GROUP
        for g in range(GROUP):
            load(at + g).wait()
        pairs = [right_sides(at + g) for g in range(GROUP)]
        for g in range(GROUP):
            pick(at + g, pairs[g])

        @pl.when(i == 0)
        def _():
            pl.semaphore_wait(barrier, evt_count - 1 + sta_count - 1)
            for j in range(1, evt_count):
                normals(j).start()

        for j in range(1, evt_count):
            remote(j, at).start()
        return carry

    lax.fori_loop(0, stations // GROUP, step, 0)

    def whole(j):
        return pltpu.make_async_remote_copy(
            src_ref=send_buf.at[lax.rem(evt + j, evt_count), :, 0:USED],
            dst_ref=recv_buf.at[j - 1, :, 0:USED],
            send_sem=send_sem.at[j - 1],
            recv_sem=recv_sem.at[j - 1],
            device_id={"evt": lax.rem(evt + j, evt_count)},
            device_id_type=pl.DeviceIdType.MESH,
        )

    row = normal_buf[0:1]
    for j in range(1, evt_count):
        normals(j).wait_recv()
        row = row + normal_recv[j - 1, 0:1]
    entries = jnp.broadcast_to(row, (stations, LANES))
    entries = jnp.where(lane_ids // TERMS == station_ids, entries, 0.0)
    matrix = {}
    place = 0
    for k in range(HARMS):
        for l in range(k + 1):
            value = jnp.sum(
                jnp.where(lane_ids % TERMS == place, entries, 0.0), axis=1, keepdims=True
            )
            value = jnp.broadcast_to(value, (stations, LANES))
            matrix[k, l] = value + 1.0 if k == l else value
            place += 1
    inverse = []
    ratio = {}
    for p in range(HARMS):
        inverse.append(1.0 / matrix[p, p])
        for k in range(p + 1, HARMS):
            ratio[k, p] = matrix[k, p] * inverse[p]
            for l in range(p + 1, k + 1):
                matrix[k, l] = matrix[k, l] - ratio[k, p] * matrix[l, p]

    sums = send_buf[evt, :, 0:USED]
    for j in range(1, evt_count):
        whole(j).wait_recv()
        sums = sums + recv_buf[j - 1, :, 0:USED]
    sum_buf[:, 0:USED] = sums
    right = [sum_buf[:, k, :] for k in range(HARMS)]
    for p in range(HARMS):
        for k in range(p + 1, HARMS):
            right[k] = right[k] - ratio[k, p] * right[p]
    solved = [None] * HARMS
    for k in reversed(range(HARMS)):
        value = right[k] * inverse[k]
        for l in range(k + 1, HARMS):
            value = value - ratio[l, k] * solved[l]
        solved[k] = value
        fit_buf[k] = solved[k]

    def fits(j):
        return pltpu.make_async_remote_copy(
            src_ref=fit_buf,
            dst_ref=fit_recv.at[j - 1],
            send_sem=fit_send_sem.at[j - 1],
            recv_sem=fit_recv_sem.at[j - 1],
            device_id={"sta": lax.rem(sta + j, sta_count)},
            device_id_type=pl.DeviceIdType.MESH,
        )

    for j in range(1, sta_count):
        fits(j).start()

    ids = lax.broadcasted_iota(jnp.int32, (stations, LANES), 0)
    masks = []
    for j in range(sta_count):
        base = lax.rem(sta + sta_count - j, sta_count) * stations
        of = jnp.zeros((stations, LANES), jnp.int32)
        for s in range(stations):
            of = jnp.where(ids == s, tile_ref[base + s], of)
        masks.append(
            [jnp.where(of == sta * tiles + t, 1.0, 0.0).astype(f32) for t in range(tiles)]
        )
    scale = []
    for t in range(tiles):
        members = functools.reduce(jnp.add, [m[t] for m in masks])
        scale.append(jnp.maximum(jnp.sum(members, axis=0, keepdims=True), 1.0))
    stack = [[masks[0][t] * solved[k] for k in range(HARMS)] for t in range(tiles)]
    for j in range(1, sta_count):
        fits(j).wait_recv()
        for k in range(HARMS):
            value = fit_recv[j - 1, k]
            for t in range(tiles):
                stack[t][k] = stack[t][k] + masks[j][t] * value
    for t in range(tiles):
        for k in range(HARMS):
            row = jnp.sum(stack[t][k], axis=0, keepdims=True) / scale[t]
            out_ref[t, k, 0:1, :] = row[:, 0:share]
            out_ref[t, k, 1:2, :] = row[:, HALF:HALF + share]
    for j in range(1, evt_count):
        whole(j).wait_send()
        normals(j).wait_send()
    for j in range(1, sta_count):
        fits(j).wait_send()


def body(evt_count, sta_count, traces, baz_bin, inc_bin, counts, depth_index, tile_of):
    _, stations, slots, samples = traces.shape
    depths = depth_index.shape[1]
    share = depths // evt_count
    pieces = -(-3 * slots // LANES)
    tiles = tile_count(tile_of.shape[0]) // sta_count
    vmem = pl.BlockSpec(memory_space=pltpu.VMEM)
    anywhere = pl.BlockSpec(memory_space=pl.ANY)
    f32 = jnp.float32
    return pl.pallas_call(
        functools.partial(kernel, evt_count, sta_count, tiles),
        out_shape=pltpu.VMEM((tiles, HARMS, 2, share), f32),
        in_specs=[anywhere] * 6,
        out_specs=vmem,
        scratch_shapes=[
            pltpu.VMEM((stations, 3, slots, samples), traces.dtype),
            pltpu.VMEM(baz_bin.shape, jnp.int32),
            pltpu.VMEM(inc_bin.shape, jnp.int32),
            pltpu.SMEM(counts.shape, jnp.int32),
            pltpu.VMEM(depth_index.shape, jnp.int32),
            pltpu.SMEM(tile_of.shape, jnp.int32),
            pltpu.VMEM((pieces, 2 * ROWS * stations, LANES), f32),
            pltpu.VMEM((stations, 4 * ROWS, pieces * LANES), jnp.bfloat16),
            pltpu.VMEM((ROWS, LANES), f32),
            pltpu.VMEM((evt_count - 1, ROWS, LANES), f32),
            pltpu.VMEM((evt_count, stations, ROWS, LANES), f32),
            pltpu.VMEM((evt_count - 1, stations, ROWS, LANES), f32),
            pltpu.VMEM((stations, ROWS, LANES), f32),
            pltpu.VMEM((HARMS, stations, LANES), f32),
            pltpu.VMEM((sta_count - 1, HARMS, stations, LANES), f32),
            pltpu.SemaphoreType.DMA((stations,)),
            pltpu.SemaphoreType.DMA((5,)),
            pltpu.SemaphoreType.DMA((evt_count - 1,)),
            pltpu.SemaphoreType.DMA((evt_count - 1,)),
            pltpu.SemaphoreType.DMA((evt_count - 1,)),
            pltpu.SemaphoreType.DMA((evt_count - 1,)),
            pltpu.SemaphoreType.DMA((sta_count - 1,)),
            pltpu.SemaphoreType.DMA((sta_count - 1,)),
        ],
        compiler_params=pltpu.CompilerParams(collective_id=0, has_side_effects=True),
    )(traces, baz_bin, inc_bin, counts, depth_index, tile_of)


def tile_count(stations):
    return stations // 2


def solution(mesh):
    return jax.shard_map(
        functools.partial(body, mesh.shape["evt"], mesh.shape["sta"]),
        mesh=mesh,
        in_specs=(
            P(None, "sta", "evt", None),
            P("sta", "evt"),
            P("sta", "evt"),
            P("sta"),
            P("sta", None),
            P(),
        ),
        out_specs=P("sta", None, None, "evt"),
        check_vma=False,
    )
```

```python
import functools

import jax
import jax.numpy as jnp
from jax import lax
from jax.experimental import pallas as pl
from jax.experimental.pallas import tpu as pltpu
from jax.sharding import PartitionSpec as P

BAZ_BINS = 36
HARMS = 5
LANES = 128
ROWS = 8
USED = HARMS
TERMS = 16
HALF = LANES // 2
GROUP = 2
CORES = 2


def pick_lanes(values, lanes):
    return jnp.take_along_axis(values, lanes, axis=1, mode="promise_in_bounds")


def kernel(
    evt_count,
    sta_count,
    tiles,
    traces_ref,
    baz_hbm,
    inc_hbm,
    counts_hbm,
    depth_hbm,
    tile_hbm,
    out_ref,
    trace_buf,
    baz_ref,
    inc_ref,
    counts_ref,
    depth_ref,
    tile_ref,
    weight_buf,
    left_buf,
    normal_buf,
    normal_recv,
    send_buf,
    pair_buf,
    relay_buf,
    recv_buf,
    sum_buf,
    fit_buf,
    fit_recv,
    load_sem,
    small_sem,
    pair_send_sem,
    pair_recv_sem,
    send_sem,
    recv_sem,
    normal_send_sem,
    normal_recv_sem,
    fit_send_sem,
    fit_recv_sem,
):
    stations, slots = baz_ref.shape
    samples = traces_ref.shape[3]
    depths = depth_ref.shape[1]
    share = depths // evt_count
    evt = lax.axis_index("evt")
    sta = lax.axis_index("sta")
    z_count = evt_count // CORES
    z_own = lax.div(evt, CORES)
    core = lax.rem(evt, CORES)
    f32 = jnp.float32

    def load(s):
        return pltpu.make_async_copy(traces_ref.at[:, s], trace_buf.at[s], load_sem.at[s])

    small = [
        pltpu.make_async_copy(src, dst, small_sem.at[n])
        for n, (src, dst) in enumerate(
            [
                (baz_hbm, baz_ref),
                (inc_hbm, inc_ref),
                (counts_hbm, counts_ref),
                (depth_hbm, depth_ref),
                (tile_hbm, tile_ref),
            ]
        )
    ]
    for copy in small:
        copy.start()
    for s in range(stations):
        load(s).start()
    barrier = pltpu.get_barrier_semaphore()
    for j in range(1, evt_count):
        pl.semaphore_signal(
            barrier, inc=1, device_id={"evt": lax.rem(evt + j, evt_count)},
            device_id_type=pl.DeviceIdType.MESH,
        )
    for j in range(1, sta_count):
        pl.semaphore_signal(
            barrier, inc=1, device_id={"sta": lax.rem(sta + j, sta_count)},
            device_id_type=pl.DeviceIdType.MESH,
        )

    for copy in small:
        copy.wait()

    phi = (baz_ref[...].astype(f32) + 0.5) * (2.0 * jnp.pi / BAZ_BINS)
    tilt = (12.0 + 2.5 * (inc_ref[...].astype(f32) + 0.5)) * (jnp.pi / 180.0)
    cosine, sine = jnp.cos(phi), jnp.sin(phi)
    cos_tilt, sin_tilt = jnp.cos(tilt), jnp.sin(tilt)
    row_ids = lax.broadcasted_iota(jnp.int32, (stations, slots), 0)
    total = jnp.zeros((stations, slots), jnp.int32)
    for s in range(stations):
        total = jnp.where(row_ids == s, counts_ref[s], total)
    slot_ids = evt * slots + lax.broadcasted_iota(jnp.int32, (stations, slots), 1)
    live = jnp.where(slot_ids < total, 1.0, 0.0).astype(f32)
    harm = [
        jnp.ones_like(phi),
        cosine,
        sine,
        2.0 * cosine * cosine - 1.0,
        2.0 * sine * cosine,
    ]
    weighted = [h * live for h in harm]
    parts = [
        [sin_tilt, -cos_tilt * cosine, -cos_tilt * sine],
        [jnp.zeros_like(phi), sine, -cosine],
    ]
    weight_buf[...] = jnp.zeros_like(weight_buf)
    for c in range(2):
        for k in range(HARMS):
            at = (c * ROWS + k) * stations
            for m in range(3):
                lane = m * slots
                weight_buf[
                    lane // LANES, at:at + stations, lane % LANES:lane % LANES + slots
                ] = weighted[k] * parts[c][m]
    for s in range(stations):
        for n in range(weight_buf.shape[0]):
            weights = weight_buf[n, pl.ds(s, 2 * ROWS, stride=stations), :]
            high = weights.astype(jnp.bfloat16)
            low = (weights - high.astype(f32)).astype(jnp.bfloat16)
            left_buf[s, 0:2 * ROWS, n * LANES:(n + 1) * LANES] = high
            left_buf[s, 2 * ROWS:4 * ROWS, n * LANES:(n + 1) * LANES] = low
    lane_ids = lax.broadcasted_iota(jnp.int32, (stations, LANES), 1)
    station_ids = lax.broadcasted_iota(jnp.int32, (stations, LANES), 0)
    packed = jnp.zeros((stations, LANES), f32)
    place = 0
    for k in range(HARMS):
        for l in range(k + 1):
            column = jnp.sum(weighted[k] * harm[l], axis=1, keepdims=True)
            packed = jnp.where(lane_ids % TERMS == place, column, packed)
            place += 1
    packed = jnp.where(lane_ids // TERMS == station_ids, packed, 0.0)
    normal_buf[0:1] = jnp.sum(packed, axis=0, keepdims=True)

    def normals(j):
        return pltpu.make_async_remote_copy(
            src_ref=normal_buf.at[0:1],
            dst_ref=normal_recv.at[j - 1, 0:1],
            send_sem=normal_send_sem.at[j - 1],
            recv_sem=normal_recv_sem.at[j - 1],
            device_id={"evt": lax.rem(evt + j, evt_count)},
            device_id_type=pl.DeviceIdType.MESH,
        )

    def to_partner(i):
        part = pl.ds(i * GROUP, GROUP)
        return pltpu.make_async_remote_copy(
            src_ref=send_buf.at[1 - core, :, part, 0:USED],
            dst_ref=pair_buf.at[:, part, 0:USED],
            send_sem=pair_send_sem.at[i],
            recv_sem=pair_recv_sem.at[i],
            device_id={"evt": z_own * CORES + 1 - core},
            device_id_type=pl.DeviceIdType.MESH,
        )

    def remote(j, first, length):
        target = lax.rem(z_own + j, z_count)
        part = pl.ds(first, length)
        return pltpu.make_async_remote_copy(
            src_ref=relay_buf.at[target, part, 0:USED],
            dst_ref=recv_buf.at[j - 1, part, 0:USED],
            send_sem=send_sem.at[j - 1],
            recv_sem=recv_sem.at[j - 1],
            device_id={"evt": target * CORES + core},
            device_id_type=pl.DeviceIdType.MESH,
        )

    def forward(i):
        to_partner(i).wait_recv()
        part = pl.ds(i * GROUP, GROUP)
        for z in range(z_count):
            relay_buf[z, part, 0:USED] = (
                send_buf[core, z, part, 0:USED] + pair_buf[z, part, 0:USED]
            )
        for j in range(1, z_count):
            remote(j, i * GROUP, GROUP).start()

    lane8 = lax.broadcasted_iota(jnp.int32, (ROWS, LANES), 1)

    def right_sides(s):
        block = trace_buf[s].reshape(3 * slots, samples)
        right = jnp.dot(left_buf[s, :, 0:3 * slots], block, preferred_element_type=f32)
        pair = right[0:2 * ROWS] + right[2 * ROWS:4 * ROWS]
        return 0.5 * (pair + pltpu.roll(pair, samples - 1, 1))

    def pick(s, pair):
        first, second = pair[0:ROWS], pair[ROWS:2 * ROWS]
        picks = depth_ref[pl.ds(s, 1), :]
        for z in range(depths // LANES):
            index = jnp.broadcast_to(picks[:, z * LANES:(z + 1) * LANES], (ROWS, LANES))
            chunk = lax.shift_right_logical(index, 7)
            lane = lax.bitwise_and(index, LANES - 1)
            got = [jnp.zeros((ROWS, LANES), f32)] * 2
            for n in range(samples // LANES):
                here = chunk == n
                for c, values in enumerate((first, second)):
                    taken = pick_lanes(values[:, n * LANES:(n + 1) * LANES], lane)
                    got[c] = jnp.where(here, taken, got[c])
            for d in range(LANES // share):
                left = got[0] if d == 0 else pltpu.roll(got[0], LANES - d * share, 1)
                move = (HALF - d * share) % LANES
                rest = got[1] if move == 0 else pltpu.roll(got[1], move, 1)
                to = z * (LANES // share) + d
                send_buf[to % CORES, to // CORES, s] = jnp.where(lane8 < HALF, left, rest)

    def step(i, carry):
        at = i * GROUP
        for g in range(GROUP):
            load(at + g).wait()
        pairs = [right_sides(at + g) for g in range(GROUP)]
        for g in range(GROUP):
            pick(at + g, pairs[g])

        @pl.when(i == 0)
        def _():
            pl.semaphore_wait(barrier, evt_count - 1 + sta_count - 1)
            for j in range(1, evt_count):
                normals(j).start()

        to_partner(i).start()

        @pl.when(i > 0)
        def _():
            forward(i - 1)

        return carry

    steps = stations // GROUP
    lax.fori_loop(0, steps, step, 0)
    forward(steps - 1)

    row = normal_buf[0:1]
    for j in range(1, evt_count):
        normals(j).wait_recv()
        row = row + normal_recv[j - 1, 0:1]
    entries = jnp.broadcast_to(row, (stations, LANES))
    entries = jnp.where(lane_ids // TERMS == station_ids, entries, 0.0)
    matrix = {}
    place = 0
    for k in range(HARMS):
        for l in range(k + 1):
            value = jnp.sum(
                jnp.where(lane_ids % TERMS == place, entries, 0.0), axis=1, keepdims=True
            )
            value = jnp.broadcast_to(value, (stations, LANES))
            matrix[k, l] = value + 1.0 if k == l else value
            place += 1
    inverse = []
    ratio = {}
    for p in range(HARMS):
        inverse.append(1.0 / matrix[p, p])
        for k in range(p + 1, HARMS):
            ratio[k, p] = matrix[k, p] * inverse[p]
            for l in range(p + 1, k + 1):
                matrix[k, l] = matrix[k, l] - ratio[k, p] * matrix[l, p]

    sums = relay_buf[z_own, :, 0:USED]
    for j in range(1, z_count):
        remote(j, 0, stations).wait_recv()
        sums = sums + recv_buf[j - 1, :, 0:USED]
    sum_buf[:, 0:USED] = sums
    right = [sum_buf[:, k, :] for k in range(HARMS)]
    for p in range(HARMS):
        for k in range(p + 1, HARMS):
            right[k] = right[k] - ratio[k, p] * right[p]
    solved = [None] * HARMS
    for k in reversed(range(HARMS)):
        value = right[k] * inverse[k]
        for l in range(k + 1, HARMS):
            value = value - ratio[l, k] * solved[l]
        solved[k] = value
        fit_buf[k] = solved[k]

    def fits(j):
        return pltpu.make_async_remote_copy(
            src_ref=fit_buf,
            dst_ref=fit_recv.at[j - 1],
            send_sem=fit_send_sem.at[j - 1],
            recv_sem=fit_recv_sem.at[j - 1],
            device_id={"sta": lax.rem(sta + j, sta_count)},
            device_id_type=pl.DeviceIdType.MESH,
        )

    for j in range(1, sta_count):
        fits(j).start()

    ids = lax.broadcasted_iota(jnp.int32, (stations, LANES), 0)
    masks = []
    for j in range(sta_count):
        base = lax.rem(sta + sta_count - j, sta_count) * stations
        of = jnp.zeros((stations, LANES), jnp.int32)
        for s in range(stations):
            of = jnp.where(ids == s, tile_ref[base + s], of)
        masks.append(
            [jnp.where(of == sta * tiles + t, 1.0, 0.0).astype(f32) for t in range(tiles)]
        )
    scale = []
    for t in range(tiles):
        members = functools.reduce(jnp.add, [m[t] for m in masks])
        scale.append(jnp.maximum(jnp.sum(members, axis=0, keepdims=True), 1.0))
    stack = [[masks[0][t] * solved[k] for k in range(HARMS)] for t in range(tiles)]
    for j in range(1, sta_count):
        fits(j).wait_recv()
        for k in range(HARMS):
            value = fit_recv[j - 1, k]
            for t in range(tiles):
                stack[t][k] = stack[t][k] + masks[j][t] * value
    for t in range(tiles):
        for k in range(HARMS):
            row = jnp.sum(stack[t][k], axis=0, keepdims=True) / scale[t]
            out_ref[t, k, 0:1, :] = row[:, 0:share]
            out_ref[t, k, 1:2, :] = row[:, HALF:HALF + share]
    for j in range(1, evt_count):
        normals(j).wait_send()
    for j in range(1, z_count):
        remote(j, 0, stations).wait_send()
    for i in range(steps):
        to_partner(i).wait_send()
    for j in range(1, sta_count):
        fits(j).wait_send()


def body(evt_count, sta_count, traces, baz_bin, inc_bin, counts, depth_index, tile_of):
    _, stations, slots, samples = traces.shape
    depths = depth_index.shape[1]
    share = depths // evt_count
    z_count = evt_count // CORES
    pieces = -(-3 * slots // LANES)
    tiles = tile_count(tile_of.shape[0]) // sta_count
    vmem = pl.BlockSpec(memory_space=pltpu.VMEM)
    anywhere = pl.BlockSpec(memory_space=pl.ANY)
    f32 = jnp.float32
    return pl.pallas_call(
        functools.partial(kernel, evt_count, sta_count, tiles),
        out_shape=pltpu.VMEM((tiles, HARMS, 2, share), f32),
        in_specs=[anywhere] * 6,
        out_specs=vmem,
        scratch_shapes=[
            pltpu.VMEM((stations, 3, slots, samples), traces.dtype),
            pltpu.VMEM(baz_bin.shape, jnp.int32),
            pltpu.VMEM(inc_bin.shape, jnp.int32),
            pltpu.SMEM(counts.shape, jnp.int32),
            pltpu.VMEM(depth_index.shape, jnp.int32),
            pltpu.SMEM(tile_of.shape, jnp.int32),
            pltpu.VMEM((pieces, 2 * ROWS * stations, LANES), f32),
            pltpu.VMEM((stations, 4 * ROWS, pieces * LANES), jnp.bfloat16),
            pltpu.VMEM((ROWS, LANES), f32),
            pltpu.VMEM((evt_count - 1, ROWS, LANES), f32),
            pltpu.VMEM((CORES, z_count, stations, ROWS, LANES), f32),
            pltpu.VMEM((z_count, stations, ROWS, LANES), f32),
            pltpu.VMEM((z_count, stations, ROWS, LANES), f32),
            pltpu.VMEM((z_count - 1, stations, ROWS, LANES), f32),
            pltpu.VMEM((stations, ROWS, LANES), f32),
            pltpu.VMEM((HARMS, stations, LANES), f32),
            pltpu.VMEM((sta_count - 1, HARMS, stations, LANES), f32),
            pltpu.SemaphoreType.DMA((stations,)),
            pltpu.SemaphoreType.DMA((5,)),
            pltpu.SemaphoreType.DMA((stations // GROUP,)),
            pltpu.SemaphoreType.DMA((stations // GROUP,)),
            pltpu.SemaphoreType.DMA((z_count - 1,)),
            pltpu.SemaphoreType.DMA((z_count - 1,)),
            pltpu.SemaphoreType.DMA((evt_count - 1,)),
            pltpu.SemaphoreType.DMA((evt_count - 1,)),
            pltpu.SemaphoreType.DMA((sta_count - 1,)),
            pltpu.SemaphoreType.DMA((sta_count - 1,)),
        ],
        compiler_params=pltpu.CompilerParams(collective_id=0, has_side_effects=True),
    )(traces, baz_bin, inc_bin, counts, depth_index, tile_of)


def tile_count(stations):
    return stations // 2


def solution(mesh):
    return jax.shard_map(
        functools.partial(body, mesh.shape["evt"], mesh.shape["sta"]),
        mesh=mesh,
        in_specs=(
            P(None, "sta", "evt", None),
            P("sta", "evt"),
            P("sta", "evt"),
            P("sta"),
            P("sta", None),
            P(),
        ),
        out_specs=P("sta", None, None, "evt"),
        check_vma=False,
    )
```

```python
import functools

import jax
import jax.numpy as jnp
from jax import lax
from jax.experimental import pallas as pl
from jax.experimental.pallas import tpu as pltpu
from jax.sharding import PartitionSpec as P

BAZ_BINS = 36
HARMS = 5
LANES = 128
ROWS = 8
USED = HARMS
TERMS = 16
HALF = LANES // 2
GROUP = 4


def pick_lanes(values, lanes):
    return jnp.take_along_axis(values, lanes, axis=1, mode="promise_in_bounds")


def kernel(
    evt_count,
    sta_count,
    tiles,
    traces_ref,
    baz_hbm,
    inc_hbm,
    counts_hbm,
    depth_hbm,
    tile_hbm,
    out_ref,
    trace_buf,
    baz_ref,
    inc_ref,
    counts_ref,
    depth_ref,
    tile_ref,
    weight_buf,
    left_buf,
    normal_buf,
    normal_recv,
    send_buf,
    recv_buf,
    sum_buf,
    fit_buf,
    fit_recv,
    load_sem,
    small_sem,
    send_sem,
    recv_sem,
    normal_send_sem,
    normal_recv_sem,
    fit_send_sem,
    fit_recv_sem,
):
    stations, slots = baz_ref.shape
    samples = traces_ref.shape[3]
    depths = depth_ref.shape[1]
    share = depths // evt_count
    evt = lax.axis_index("evt")
    sta = lax.axis_index("sta")
    f32 = jnp.float32

    def load(s):
        return pltpu.make_async_copy(traces_ref.at[:, s], trace_buf.at[s], load_sem.at[s])

    small = [
        pltpu.make_async_copy(src, dst, small_sem.at[n])
        for n, (src, dst) in enumerate(
            [
                (baz_hbm, baz_ref),
                (inc_hbm, inc_ref),
                (counts_hbm, counts_ref),
                (depth_hbm, depth_ref),
                (tile_hbm, tile_ref),
            ]
        )
    ]
    for copy in small:
        copy.start()
    for s in range(stations):
        load(s).start()
    barrier = pltpu.get_barrier_semaphore()
    for j in range(1, evt_count):
        pl.semaphore_signal(
            barrier, inc=1, device_id={"evt": lax.rem(evt + j, evt_count)},
            device_id_type=pl.DeviceIdType.MESH,
        )
    for j in range(1, sta_count):
        pl.semaphore_signal(
            barrier, inc=1, device_id={"sta": lax.rem(sta + j, sta_count)},
            device_id_type=pl.DeviceIdType.MESH,
        )

    for copy in small:
        copy.wait()

    phi = (baz_ref[...].astype(f32) + 0.5) * (2.0 * jnp.pi / BAZ_BINS)
    tilt = (12.0 + 2.5 * (inc_ref[...].astype(f32) + 0.5)) * (jnp.pi / 180.0)
    cosine, sine = jnp.cos(phi), jnp.sin(phi)
    cos_tilt, sin_tilt = jnp.cos(tilt), jnp.sin(tilt)
    row_ids = lax.broadcasted_iota(jnp.int32, (stations, slots), 0)
    total = jnp.zeros((stations, slots), jnp.int32)
    for s in range(stations):
        total = jnp.where(row_ids == s, counts_ref[s], total)
    slot_ids = evt * slots + lax.broadcasted_iota(jnp.int32, (stations, slots), 1)
    live = jnp.where(slot_ids < total, 1.0, 0.0).astype(f32)
    harm = [
        jnp.ones_like(phi),
        cosine,
        sine,
        2.0 * cosine * cosine - 1.0,
        2.0 * sine * cosine,
    ]
    weighted = [h * live for h in harm]
    parts = [
        [sin_tilt, -cos_tilt * cosine, -cos_tilt * sine],
        [jnp.zeros_like(phi), sine, -cosine],
    ]
    weight_buf[...] = jnp.zeros_like(weight_buf)
    for c in range(2):
        for k in range(HARMS):
            at = (c * ROWS + k) * stations
            for m in range(3):
                lane = m * slots
                weight_buf[
                    lane // LANES, at:at + stations, lane % LANES:lane % LANES + slots
                ] = weighted[k] * parts[c][m]
    for s in range(stations):
        for n in range(weight_buf.shape[0]):
            weights = weight_buf[n, pl.ds(s, 2 * ROWS, stride=stations), :]
            high = weights.astype(jnp.bfloat16)
            low = (weights - high.astype(f32)).astype(jnp.bfloat16)
            left_buf[s, 0:2 * ROWS, n * LANES:(n + 1) * LANES] = high
            left_buf[s, 2 * ROWS:4 * ROWS, n * LANES:(n + 1) * LANES] = low
    lane_ids = lax.broadcasted_iota(jnp.int32, (stations, LANES), 1)
    station_ids = lax.broadcasted_iota(jnp.int32, (stations, LANES), 0)
    packed = jnp.zeros((stations, LANES), f32)
    place = 0
    for k in range(HARMS):
        for l in range(k + 1):
            column = jnp.sum(weighted[k] * harm[l], axis=1, keepdims=True)
            packed = jnp.where(lane_ids % TERMS == place, column, packed)
            place += 1
    packed = jnp.where(lane_ids // TERMS == station_ids, packed, 0.0)
    normal_buf[0:1] = jnp.sum(packed, axis=0, keepdims=True)

    def normals(j):
        return pltpu.make_async_remote_copy(
            src_ref=normal_buf.at[0:1],
            dst_ref=normal_recv.at[j - 1, 0:1],
            send_sem=normal_send_sem.at[j - 1],
            recv_sem=normal_recv_sem.at[j - 1],
            device_id={"evt": lax.rem(evt + j, evt_count)},
            device_id_type=pl.DeviceIdType.MESH,
        )

    def remote(j, s):
        target = lax.rem(evt + j, evt_count)
        return pltpu.make_async_remote_copy(
            src_ref=send_buf.at[target, pl.ds(s, GROUP), 0:USED],
            dst_ref=recv_buf.at[j - 1, pl.ds(s, GROUP), 0:USED],
            send_sem=send_sem.at[j - 1],
            recv_sem=recv_sem.at[j - 1],
            device_id={"evt": target},
            device_id_type=pl.DeviceIdType.MESH,
        )

    lane8 = lax.broadcasted_iota(jnp.int32, (ROWS, LANES), 1)

    def right_sides(s):
        block = trace_buf[s].reshape(3 * slots, samples)
        right = jnp.dot(left_buf[s, :, 0:3 * slots], block, preferred_element_type=f32)
        pair = right[0:2 * ROWS] + right[2 * ROWS:4 * ROWS]
        return 0.5 * (pair + pltpu.roll(pair, samples - 1, 1))

    def pick(s, pair):
        first, second = pair[0:ROWS], pair[ROWS:2 * ROWS]
        picks = depth_ref[pl.ds(s, 1), :]
        for z in range(depths // LANES):
            index = jnp.broadcast_to(picks[:, z * LANES:(z + 1) * LANES], (ROWS, LANES))
            chunk = lax.shift_right_logical(index, 7)
            lane = lax.bitwise_and(index, LANES - 1)
            got = [jnp.zeros((ROWS, LANES), f32)] * 2
            for n in range(samples // LANES):
                here = chunk == n
                for c, values in enumerate((first, second)):
                    taken = pick_lanes(values[:, n * LANES:(n + 1) * LANES], lane)
                    got[c] = jnp.where(here, taken, got[c])
            for d in range(LANES // share):
                left = got[0] if d == 0 else pltpu.roll(got[0], LANES - d * share, 1)
                move = (HALF - d * share) % LANES
                rest = got[1] if move == 0 else pltpu.roll(got[1], move, 1)
                send_buf[z * (LANES // share) + d, s] = jnp.where(lane8 < HALF, left, rest)

    def step(i, carry):
        at = i * GROUP
        for g in range(GROUP):
            load(at + g).wait()
        pairs = [right_sides(at + g) for g in range(GROUP)]
        for g in range(GROUP):
            pick(at + g, pairs[g])

        @pl.when(i == 0)
        def _():
            pl.semaphore_wait(barrier, evt_count - 1 + sta_count - 1)
            for j in range(1, evt_count):
                normals(j).start()

        for j in range(1, evt_count):
            remote(j, at).start()
        return carry

    lax.fori_loop(0, stations // GROUP, step, 0)

    def whole(j):
        return pltpu.make_async_remote_copy(
            src_ref=send_buf.at[lax.rem(evt + j, evt_count), :, 0:USED],
            dst_ref=recv_buf.at[j - 1, :, 0:USED],
            send_sem=send_sem.at[j - 1],
            recv_sem=recv_sem.at[j - 1],
            device_id={"evt": lax.rem(evt + j, evt_count)},
            device_id_type=pl.DeviceIdType.MESH,
        )

    row = normal_buf[0:1]
    for j in range(1, evt_count):
        normals(j).wait_recv()
        row = row + normal_recv[j - 1, 0:1]
    entries = jnp.broadcast_to(row, (stations, LANES))
    entries = jnp.where(lane_ids // TERMS == station_ids, entries, 0.0)
    matrix = {}
    place = 0
    for k in range(HARMS):
        for l in range(k + 1):
            value = jnp.sum(
                jnp.where(lane_ids % TERMS == place, entries, 0.0), axis=1, keepdims=True
            )
            value = jnp.broadcast_to(value, (stations, LANES))
            matrix[k, l] = value + 1.0 if k == l else value
            place += 1
    inverse = []
    ratio = {}
    for p in range(HARMS):
        inverse.append(1.0 / matrix[p, p])
        for k in range(p + 1, HARMS):
            ratio[k, p] = matrix[k, p] * inverse[p]
            for l in range(p + 1, k + 1):
                matrix[k, l] = matrix[k, l] - ratio[k, p] * matrix[l, p]

    sums = send_buf[evt, :, 0:USED]
    for j in range(1, evt_count):
        whole(j).wait_recv()
        sums = sums + recv_buf[j - 1, :, 0:USED]
    sum_buf[:, 0:USED] = sums
    right = [sum_buf[:, k, :] for k in range(HARMS)]
    for p in range(HARMS):
        for k in range(p + 1, HARMS):
            right[k] = right[k] - ratio[k, p] * right[p]
    solved = [None] * HARMS
    for k in reversed(range(HARMS)):
        value = right[k] * inverse[k]
        for l in range(k + 1, HARMS):
            value = value - ratio[l, k] * solved[l]
        solved[k] = value
        fit_buf[k] = solved[k]

    def fits(j):
        return pltpu.make_async_remote_copy(
            src_ref=fit_buf,
            dst_ref=fit_recv.at[j - 1],
            send_sem=fit_send_sem.at[j - 1],
            recv_sem=fit_recv_sem.at[j - 1],
            device_id={"sta": lax.rem(sta + j, sta_count)},
            device_id_type=pl.DeviceIdType.MESH,
        )

    for j in range(1, sta_count):
        fits(j).start()

    ids = lax.broadcasted_iota(jnp.int32, (stations, LANES), 0)
    masks = []
    for j in range(sta_count):
        base = lax.rem(sta + sta_count - j, sta_count) * stations
        of = jnp.zeros((stations, LANES), jnp.int32)
        for s in range(stations):
            of = jnp.where(ids == s, tile_ref[base + s], of)
        masks.append(
            [jnp.where(of == sta * tiles + t, 1.0, 0.0).astype(f32) for t in range(tiles)]
        )
    scale = []
    for t in range(tiles):
        members = functools.reduce(jnp.add, [m[t] for m in masks])
        scale.append(jnp.maximum(jnp.sum(members, axis=0, keepdims=True), 1.0))
    stack = [[masks[0][t] * solved[k] for k in range(HARMS)] for t in range(tiles)]
    for j in range(1, sta_count):
        fits(j).wait_recv()
        for k in range(HARMS):
            value = fit_recv[j - 1, k]
            for t in range(tiles):
                stack[t][k] = stack[t][k] + masks[j][t] * value
    for t in range(tiles):
        for k in range(HARMS):
            row = jnp.sum(stack[t][k], axis=0, keepdims=True) / scale[t]
            out_ref[t, k, 0:1, :] = row[:, 0:share]
            out_ref[t, k, 1:2, :] = row[:, HALF:HALF + share]
    for j in range(1, evt_count):
        whole(j).wait_send()
        normals(j).wait_send()
    for j in range(1, sta_count):
        fits(j).wait_send()


def body(evt_count, sta_count, traces, baz_bin, inc_bin, counts, depth_index, tile_of):
    _, stations, slots, samples = traces.shape
    depths = depth_index.shape[1]
    share = depths // evt_count
    pieces = -(-3 * slots // LANES)
    tiles = tile_count(tile_of.shape[0]) // sta_count
    vmem = pl.BlockSpec(memory_space=pltpu.VMEM)
    anywhere = pl.BlockSpec(memory_space=pl.ANY)
    f32 = jnp.float32
    return pl.pallas_call(
        functools.partial(kernel, evt_count, sta_count, tiles),
        out_shape=pltpu.VMEM((tiles, HARMS, 2, share), f32),
        in_specs=[anywhere] * 6,
        out_specs=vmem,
        scratch_shapes=[
            pltpu.VMEM((stations, 3, slots, samples), traces.dtype),
            pltpu.VMEM(baz_bin.shape, jnp.int32),
            pltpu.VMEM(inc_bin.shape, jnp.int32),
            pltpu.SMEM(counts.shape, jnp.int32),
            pltpu.VMEM(depth_index.shape, jnp.int32),
            pltpu.SMEM(tile_of.shape, jnp.int32),
            pltpu.VMEM((pieces, 2 * ROWS * stations, LANES), f32),
            pltpu.VMEM((stations, 4 * ROWS, pieces * LANES), jnp.bfloat16),
            pltpu.VMEM((ROWS, LANES), f32),
            pltpu.VMEM((evt_count - 1, ROWS, LANES), f32),
            pltpu.VMEM((evt_count, stations, ROWS, LANES), f32),
            pltpu.VMEM((evt_count - 1, stations, ROWS, LANES), f32),
            pltpu.VMEM((stations, ROWS, LANES), f32),
            pltpu.VMEM((HARMS, stations, LANES), f32),
            pltpu.VMEM((sta_count - 1, HARMS, stations, LANES), f32),
            pltpu.SemaphoreType.DMA((stations,)),
            pltpu.SemaphoreType.DMA((5,)),
            pltpu.SemaphoreType.DMA((evt_count - 1,)),
            pltpu.SemaphoreType.DMA((evt_count - 1,)),
            pltpu.SemaphoreType.DMA((evt_count - 1,)),
            pltpu.SemaphoreType.DMA((evt_count - 1,)),
            pltpu.SemaphoreType.DMA((sta_count - 1,)),
            pltpu.SemaphoreType.DMA((sta_count - 1,)),
        ],
        compiler_params=pltpu.CompilerParams(collective_id=0, has_side_effects=True),
    )(traces, baz_bin, inc_bin, counts, depth_index, tile_of)


def tile_count(stations):
    return stations // 2


def solution(mesh):
    return jax.shard_map(
        functools.partial(body, mesh.shape["evt"], mesh.shape["sta"]),
        mesh=mesh,
        in_specs=(
            P(None, "sta", "evt", None),
            P("sta", "evt"),
            P("sta", "evt"),
            P("sta"),
            P("sta", None),
            P(),
        ),
        out_specs=P("sta", None, None, "evt"),
        check_vma=False,
    )
```

```python
import functools

import jax
import jax.numpy as jnp
from jax import lax
from jax.experimental import pallas as pl
from jax.experimental.pallas import tpu as pltpu
from jax.sharding import PartitionSpec as P

BAZ_BINS = 36
HARMS = 5
LANES = 128
ROWS = 8
USED = HARMS
TERMS = 16
HALF = LANES // 2
GROUP = 4


def pick_lanes(values, lanes):
    return jnp.take_along_axis(values, lanes, axis=1, mode="promise_in_bounds")


def kernel(
    evt_count,
    sta_count,
    tiles,
    traces_ref,
    baz_hbm,
    inc_hbm,
    counts_hbm,
    depth_hbm,
    tile_hbm,
    out_ref,
    trace_buf,
    baz_ref,
    inc_ref,
    counts_ref,
    depth_ref,
    tile_ref,
    weight_buf,
    left_buf,
    normal_buf,
    normal_recv,
    send_buf,
    recv_buf,
    sum_buf,
    fit_buf,
    fit_recv,
    load_sem,
    small_sem,
    send_sem,
    recv_sem,
    normal_send_sem,
    normal_recv_sem,
    fit_send_sem,
    fit_recv_sem,
):
    stations, slots = baz_ref.shape
    samples = traces_ref.shape[3]
    depths = depth_ref.shape[1]
    share = depths // evt_count
    evt = lax.axis_index("evt")
    sta = lax.axis_index("sta")
    f32 = jnp.float32

    def load(s):
        return pltpu.make_async_copy(traces_ref.at[:, s], trace_buf.at[s], load_sem.at[s])

    small = [
        pltpu.make_async_copy(src, dst, small_sem.at[n])
        for n, (src, dst) in enumerate(
            [
                (baz_hbm, baz_ref),
                (inc_hbm, inc_ref),
                (counts_hbm, counts_ref),
                (depth_hbm, depth_ref),
                (tile_hbm, tile_ref),
            ]
        )
    ]
    for copy in small:
        copy.start()
    for s in range(stations):
        load(s).start()
    barrier = pltpu.get_barrier_semaphore()
    for j in range(1, evt_count):
        pl.semaphore_signal(
            barrier, inc=1, device_id={"evt": lax.rem(evt + j, evt_count)},
            device_id_type=pl.DeviceIdType.MESH,
        )
    for j in range(1, sta_count):
        pl.semaphore_signal(
            barrier, inc=1, device_id={"sta": lax.rem(sta + j, sta_count)},
            device_id_type=pl.DeviceIdType.MESH,
        )

    for copy in small:
        copy.wait()

    phi = (baz_ref[...].astype(f32) + 0.5) * (2.0 * jnp.pi / BAZ_BINS)
    tilt = (12.0 + 2.5 * (inc_ref[...].astype(f32) + 0.5)) * (jnp.pi / 180.0)
    cosine, sine = jnp.cos(phi), jnp.sin(phi)
    cos_tilt, sin_tilt = jnp.cos(tilt), jnp.sin(tilt)
    row_ids = lax.broadcasted_iota(jnp.int32, (stations, slots), 0)
    total = jnp.zeros((stations, slots), jnp.int32)
    for s in range(stations):
        total = jnp.where(row_ids == s, counts_ref[s], total)
    slot_ids = evt * slots + lax.broadcasted_iota(jnp.int32, (stations, slots), 1)
    live = jnp.where(slot_ids < total, 1.0, 0.0).astype(f32)
    harm = [
        jnp.ones_like(phi),
        cosine,
        sine,
        2.0 * cosine * cosine - 1.0,
        2.0 * sine * cosine,
    ]
    weighted = [h * live for h in harm]
    parts = [
        [sin_tilt, -cos_tilt * cosine, -cos_tilt * sine],
        [jnp.zeros_like(phi), sine, -cosine],
    ]
    weight_buf[...] = jnp.zeros_like(weight_buf)
    for c in range(2):
        for k in range(HARMS):
            at = (c * ROWS + k) * stations
            for m in range(3):
                lane = m * slots
                weight_buf[
                    lane // LANES, at:at + stations, lane % LANES:lane % LANES + slots
                ] = weighted[k] * parts[c][m]
    for s in range(stations):
        for n in range(weight_buf.shape[0]):
            weights = weight_buf[n, pl.ds(s, 2 * ROWS, stride=stations), :]
            high = weights.astype(jnp.bfloat16)
            low = (weights - high.astype(f32)).astype(jnp.bfloat16)
            left_buf[s, 0:2 * ROWS, n * LANES:(n + 1) * LANES] = high
            left_buf[s, 2 * ROWS:4 * ROWS, n * LANES:(n + 1) * LANES] = low
    lane_ids = lax.broadcasted_iota(jnp.int32, (stations, LANES), 1)
    station_ids = lax.broadcasted_iota(jnp.int32, (stations, LANES), 0)
    packed = jnp.zeros((stations, LANES), f32)
    place = 0
    for k in range(HARMS):
        for l in range(k + 1):
            column = jnp.sum(weighted[k] * harm[l], axis=1, keepdims=True)
            packed = jnp.where(lane_ids % TERMS == place, column, packed)
            place += 1
    packed = jnp.where(lane_ids // TERMS == station_ids, packed, 0.0)
    normal_buf[0:1] = jnp.sum(packed, axis=0, keepdims=True)

    def normals(j):
        return pltpu.make_async_remote_copy(
            src_ref=normal_buf.at[0:1],
            dst_ref=normal_recv.at[j - 1, 0:1],
            send_sem=normal_send_sem.at[j - 1],
            recv_sem=normal_recv_sem.at[j - 1],
            device_id={"evt": lax.rem(evt + j, evt_count)},
            device_id_type=pl.DeviceIdType.MESH,
        )

    def remote(j, s):
        target = lax.rem(evt + j, evt_count)
        return pltpu.make_async_remote_copy(
            src_ref=send_buf.at[target, pl.ds(s, GROUP), 0:USED],
            dst_ref=recv_buf.at[j - 1, pl.ds(s, GROUP), 0:USED],
            send_sem=send_sem.at[j - 1],
            recv_sem=recv_sem.at[j - 1],
            device_id={"evt": target},
            device_id_type=pl.DeviceIdType.MESH,
        )

    lane8 = lax.broadcasted_iota(jnp.int32, (ROWS, LANES), 1)

    def right_sides(s):
        block = trace_buf[s].reshape(3 * slots, samples)
        right = jnp.dot(left_buf[s, :, 0:3 * slots], block, preferred_element_type=f32)
        pair = right[0:2 * ROWS] + right[2 * ROWS:4 * ROWS]
        return 0.5 * (pair + pltpu.roll(pair, samples - 1, 1))

    def pick(s, pair):
        first, second = pair[0:ROWS], pair[ROWS:2 * ROWS]
        picks = depth_ref[pl.ds(s, 1), :]
        for z in range(depths // LANES):
            index = jnp.broadcast_to(picks[:, z * LANES:(z + 1) * LANES], (ROWS, LANES))
            chunk = lax.shift_right_logical(index, 7)
            lane = lax.bitwise_and(index, LANES - 1)
            got = [jnp.zeros((ROWS, LANES), f32)] * 2
            for n in range(samples // LANES):
                here = chunk == n
                for c, values in enumerate((first, second)):
                    taken = pick_lanes(values[:, n * LANES:(n + 1) * LANES], lane)
                    got[c] = jnp.where(here, taken, got[c])
            for d in range(LANES // share):
                left = got[0] if d == 0 else pltpu.roll(got[0], LANES - d * share, 1)
                move = (HALF - d * share) % LANES
                rest = got[1] if move == 0 else pltpu.roll(got[1], move, 1)
                send_buf[z * (LANES // share) + d, s] = jnp.where(lane8 < HALF, left, rest)

    def step(i, carry):
        at = i * GROUP
        pairs = []
        for g in range(GROUP):
            load(at + g).wait()
            pairs.append(right_sides(at + g))
        for g in range(GROUP):
            pick(at + g, pairs[g])

        @pl.when(i == 0)
        def _():
            pl.semaphore_wait(barrier, evt_count - 1 + sta_count - 1)
            for j in range(1, evt_count):
                normals(j).start()

        for j in range(1, evt_count):
            remote(j, at).start()
        return carry

    lax.fori_loop(0, stations // GROUP, step, 0)

    def whole(j):
        return pltpu.make_async_remote_copy(
            src_ref=send_buf.at[lax.rem(evt + j, evt_count), :, 0:USED],
            dst_ref=recv_buf.at[j - 1, :, 0:USED],
            send_sem=send_sem.at[j - 1],
            recv_sem=recv_sem.at[j - 1],
            device_id={"evt": lax.rem(evt + j, evt_count)},
            device_id_type=pl.DeviceIdType.MESH,
        )

    row = normal_buf[0:1]
    for j in range(1, evt_count):
        normals(j).wait_recv()
        row = row + normal_recv[j - 1, 0:1]
    entries = jnp.broadcast_to(row, (stations, LANES))
    entries = jnp.where(lane_ids // TERMS == station_ids, entries, 0.0)
    matrix = {}
    place = 0
    for k in range(HARMS):
        for l in range(k + 1):
            value = jnp.sum(
                jnp.where(lane_ids % TERMS == place, entries, 0.0), axis=1, keepdims=True
            )
            value = jnp.broadcast_to(value, (stations, LANES))
            matrix[k, l] = value + 1.0 if k == l else value
            place += 1
    inverse = []
    ratio = {}
    for p in range(HARMS):
        inverse.append(1.0 / matrix[p, p])
        for k in range(p + 1, HARMS):
            ratio[k, p] = matrix[k, p] * inverse[p]
            for l in range(p + 1, k + 1):
                matrix[k, l] = matrix[k, l] - ratio[k, p] * matrix[l, p]

    sums = send_buf[evt, :, 0:USED]
    for j in range(1, evt_count):
        whole(j).wait_recv()
        sums = sums + recv_buf[j - 1, :, 0:USED]
    sum_buf[:, 0:USED] = sums
    right = [sum_buf[:, k, :] for k in range(HARMS)]
    for p in range(HARMS):
        for k in range(p + 1, HARMS):
            right[k] = right[k] - ratio[k, p] * right[p]
    solved = [None] * HARMS
    for k in reversed(range(HARMS)):
        value = right[k] * inverse[k]
        for l in range(k + 1, HARMS):
            value = value - ratio[l, k] * solved[l]
        solved[k] = value
        fit_buf[k] = solved[k]

    def fits(j):
        return pltpu.make_async_remote_copy(
            src_ref=fit_buf,
            dst_ref=fit_recv.at[j - 1],
            send_sem=fit_send_sem.at[j - 1],
            recv_sem=fit_recv_sem.at[j - 1],
            device_id={"sta": lax.rem(sta + j, sta_count)},
            device_id_type=pl.DeviceIdType.MESH,
        )

    for j in range(1, sta_count):
        fits(j).start()

    ids = lax.broadcasted_iota(jnp.int32, (stations, LANES), 0)
    masks = []
    for j in range(sta_count):
        base = lax.rem(sta + sta_count - j, sta_count) * stations
        of = jnp.zeros((stations, LANES), jnp.int32)
        for s in range(stations):
            of = jnp.where(ids == s, tile_ref[base + s], of)
        masks.append(
            [jnp.where(of == sta * tiles + t, 1.0, 0.0).astype(f32) for t in range(tiles)]
        )
    scale = []
    for t in range(tiles):
        members = functools.reduce(jnp.add, [m[t] for m in masks])
        scale.append(jnp.maximum(jnp.sum(members, axis=0, keepdims=True), 1.0))
    stack = [[masks[0][t] * solved[k] for k in range(HARMS)] for t in range(tiles)]
    for j in range(1, sta_count):
        fits(j).wait_recv()
        for k in range(HARMS):
            value = fit_recv[j - 1, k]
            for t in range(tiles):
                stack[t][k] = stack[t][k] + masks[j][t] * value
    for t in range(tiles):
        for k in range(HARMS):
            row = jnp.sum(stack[t][k], axis=0, keepdims=True) / scale[t]
            out_ref[t, k, 0:1, :] = row[:, 0:share]
            out_ref[t, k, 1:2, :] = row[:, HALF:HALF + share]
    for j in range(1, evt_count):
        whole(j).wait_send()
        normals(j).wait_send()
    for j in range(1, sta_count):
        fits(j).wait_send()


def body(evt_count, sta_count, traces, baz_bin, inc_bin, counts, depth_index, tile_of):
    _, stations, slots, samples = traces.shape
    depths = depth_index.shape[1]
    share = depths // evt_count
    pieces = -(-3 * slots // LANES)
    tiles = tile_count(tile_of.shape[0]) // sta_count
    vmem = pl.BlockSpec(memory_space=pltpu.VMEM)
    anywhere = pl.BlockSpec(memory_space=pl.ANY)
    f32 = jnp.float32
    return pl.pallas_call(
        functools.partial(kernel, evt_count, sta_count, tiles),
        out_shape=pltpu.VMEM((tiles, HARMS, 2, share), f32),
        in_specs=[anywhere] * 6,
        out_specs=vmem,
        scratch_shapes=[
            pltpu.VMEM((stations, 3, slots, samples), traces.dtype),
            pltpu.VMEM(baz_bin.shape, jnp.int32),
            pltpu.VMEM(inc_bin.shape, jnp.int32),
            pltpu.SMEM(counts.shape, jnp.int32),
            pltpu.VMEM(depth_index.shape, jnp.int32),
            pltpu.SMEM(tile_of.shape, jnp.int32),
            pltpu.VMEM((pieces, 2 * ROWS * stations, LANES), f32),
            pltpu.VMEM((stations, 4 * ROWS, pieces * LANES), jnp.bfloat16),
            pltpu.VMEM((ROWS, LANES), f32),
            pltpu.VMEM((evt_count - 1, ROWS, LANES), f32),
            pltpu.VMEM((evt_count, stations, ROWS, LANES), f32),
            pltpu.VMEM((evt_count - 1, stations, ROWS, LANES), f32),
            pltpu.VMEM((stations, ROWS, LANES), f32),
            pltpu.VMEM((HARMS, stations, LANES), f32),
            pltpu.VMEM((sta_count - 1, HARMS, stations, LANES), f32),
            pltpu.SemaphoreType.DMA((stations,)),
            pltpu.SemaphoreType.DMA((5,)),
            pltpu.SemaphoreType.DMA((evt_count - 1,)),
            pltpu.SemaphoreType.DMA((evt_count - 1,)),
            pltpu.SemaphoreType.DMA((evt_count - 1,)),
            pltpu.SemaphoreType.DMA((evt_count - 1,)),
            pltpu.SemaphoreType.DMA((sta_count - 1,)),
            pltpu.SemaphoreType.DMA((sta_count - 1,)),
        ],
        compiler_params=pltpu.CompilerParams(collective_id=0, has_side_effects=True),
    )(traces, baz_bin, inc_bin, counts, depth_index, tile_of)


def tile_count(stations):
    return stations // 2


def solution(mesh):
    return jax.shard_map(
        functools.partial(body, mesh.shape["evt"], mesh.shape["sta"]),
        mesh=mesh,
        in_specs=(
            P(None, "sta", "evt", None),
            P("sta", "evt"),
            P("sta", "evt"),
            P("sta"),
            P("sta", None),
            P(),
        ),
        out_specs=P("sta", None, None, "evt"),
        check_vma=False,
    )
```
